128 devices in a mesh: gx: 8 (over x_lo, z), gy: 16 (over y, x_hi, core).
Axes of the slice: x: 4 (x_hi: 2, x_lo: 2; x = x_hi * 2 + x_lo), y: 4, z: 4, core: 2. Of those that a mesh axis runs over, the one named last changes fastest.
Arguments:
- populations_in: float32 [19, 4, 256, 6144], P(None, None, 'gx', 'gy'), may hold values from 0.02 to 0.1
- marker_force: float32 [2, 3, 65536], P(None, None, ('gx', 'gy')), may hold values from -1.2 to 1.2
- marker_frac: float32 [2, 3, 65536], P(None, None, ('gx', 'gy')), may hold values from 0 to 1
- marker_cell: int32 [2, 3, 65536], P(None, None, ('gx', 'gy')), may hold values from 0 to 382, as said below
- marker_tile: int32 [2, 65536, 1], P(None, ('gx', 'gy')), may hold values from 0 to 127; in each aligned block of 512 rows (0 to 511, 512 to 1023, ..., all dimensions but the last counted through in order) at most 8 rows name the same one
Outputs:
- populations_out: float32 [19, 4, 256, 6144], P(None, None, 'gx', 'gy')
- marker_velocity: float32 [2, 3, 65536], P(None, None, ('gx', 'gy'))
The draws below stay inside these ranges and needn't reach their ends.
Inputs may be any that keep to these rules, and one draw needn't show every extreme that they name: `marker_cell`: row 0 lies below 31, row 1 below 383, row 2 below 3, so that a marker's 2 x 2 x 2 kernel stays inside the tile that marker_tile names. `marker_tile`: in each step, of the 512 markers that one device holds at most 8 name the same tile.
All inputs are finite; a program needn't handle non-finite values.
Results may differ from the reference program's by a relative error of at most 0.0003.
Values sent between devices are 32-bit elements; how exact they have to be, the bound alone decides.
A program may use at most 128 MiB of HBM per device.

```python
import math
import jax
import jax.numpy as jnp
import numpy as np

VELOCITIES = 19
PLANES = 4
STEPS = 2
CX = 32
CY = 384
MK_DEV = 512
MARKERS = 65536
CAP = 8
NX = 256
NY = 6144
N_GY = 16
DEVICES = 128


def draw_marker_cell(key, part):
    upper = jnp.array([CX - 1, CY - 1, PLANES - 1], jnp.int32)
    return jax.random.randint(key, (STEPS, 3, MARKERS), 0, upper[None, :, None]).astype(jnp.int32)


def block_scale(rng, dims, shards, least, high):
    factor_of, own = 1.0, jax.random.fold_in(rng, 6)
    for position, blocks in shards:
        draws = jnp.exp(jax.random.uniform(jax.random.fold_in(own, position), (blocks,), jnp.float32, least / len(shards), high / len(shards)))
        factor_of = factor_of * jnp.repeat(draws, dims[position] // blocks).reshape([-1 if axis == position else 1 for axis in range(len(dims))])
    return factor_of


def assign_block(rng, own, number, rows, count, top, most, skew):
    sequence = jax.random.permutation(rng, count)
    crowded, ordinary = shares(count, rows * top, most, skew, True), shares(count, rows * top, most, skew, False)
    places = jnp.arange(count)

    def named(sizes, offset_by):
        used = int((sizes > 0).sum())
        fixed = max(1, used // 4)
        passed = fixed + (places - fixed + offset_by * (used - fixed)) % max(1, count - fixed)
        return jnp.zeros((count,), jnp.int32).at[sequence[jnp.where(places < fixed, places, passed)]].set(jnp.asarray(sizes, jnp.int32))

    sizes = jnp.where(number % 4 == 0, named(crowded, number // 4), named(ordinary, number - number // 4 - 1))
    mixed = jax.random.permutation(jax.random.fold_in(own, 3), count)
    source_of, sink = mixed[0:count // 2 * 2:2], mixed[1:count // 2 * 2:2]
    margin = jnp.minimum(sizes[source_of] - 1, most - sizes[sink]) // 2
    margin = jnp.where((source_of == sequence[0]) | (sink == sequence[0]) | (sizes[sink] == 0), 0, jnp.maximum(margin, 0))
    passed = jax.random.randint(jax.random.fold_in(own, 4), (count // 2,), 0, 1 << 20) % (margin + 1)
    sizes = sizes.at[source_of].add(-passed).at[sink].add(passed)
    members = jnp.searchsorted(jnp.cumsum(sizes), jnp.arange(rows * top), side="right").astype(jnp.int32)
    table = members.reshape(top, rows).T
    table = table[jax.random.permutation(jax.random.fold_in(own, 1), rows)]
    offset_by = jax.random.randint(jax.random.fold_in(own, 2), (rows, 1), 0, top)
    return jnp.take_along_axis(table, (jnp.arange(top)[None, :] + offset_by) % top, axis=1)


def shares(number_of, total, reach, slope, full):
    weights = [(1 << 20) // math.isqrt(rank ** slope) + 1 for rank in range(1, number_of + 1)]
    largest = reach if full else min(reach, max(-(-total // number_of), total * weights[0] // sum(weights)))
    least = 1 if total - largest >= number_of - 1 else 0
    holding, surplus = [largest] + [least] * (number_of - 1), total - largest - least * (number_of - 1)
    while surplus > 0:
        candidates = [i for i in range(1, number_of) if holding[i] < largest] or [i for i in range(1, number_of) if holding[i] < reach]
        pool, budget = sum([weights[i] for i in candidates]), surplus
        for i in candidates:
            more = min(reach - holding[i], max(1, budget * weights[i] // pool), surplus)
            holding[i] = holding[i] + more
            surplus = surplus - more
    return np.array(holding)


def bell_draw(stream_key, shape, deviation, bound, cuts=(), kind=jnp.bfloat16):
    values = jax.random.normal(stream_key, shape, jnp.float32) * deviation
    if len(cuts) > 0:
        values = block_scale(stream_key, shape, cuts, -0.22, 0.18) * values
    return jnp.clip(values, min=-bound, max=bound).astype(kind)


def setup_inputs(seed: int = 0) -> dict:
    streams_of = jax.random.split(jax.random.key(seed), 6)
    populations_in = jnp.clip(0.02 + 0.08 * jax.random.uniform(streams_of[0], (VELOCITIES, PLANES, NX, NY), jnp.float32) ** block_scale(streams_of[0], (VELOCITIES, PLANES, NX, NY), ((2, 8), (3, 16)), -0.2, 0.2), 0.02, 0.1)
    marker_force = bell_draw(streams_of[1], (STEPS, 3, MARKERS), 0.2, 1.2, ((2, 128),), jnp.float32)
    marker_frac = jnp.clip(1.0 * jax.random.uniform(streams_of[2], (STEPS, 3, MARKERS), jnp.float32) ** block_scale(streams_of[2], (STEPS, 3, MARKERS), ((2, 128),), -0.2, 0.2), 0.0, 1.0)
    marker_cell = draw_marker_cell(jax.random.fold_in(streams_of[5], 71), 0)
    marker_tile_keys = jax.random.split(jax.random.fold_in(streams_of[4], 1), STEPS * MARKERS // MK_DEV)
    marker_tile_turns = jax.random.permutation(jax.random.fold_in(streams_of[4], 3), STEPS * MARKERS // MK_DEV)
    marker_tile = jax.vmap(lambda own, number: assign_block(jax.random.fold_in(streams_of[4], 2), own, number, MK_DEV, DEVICES, 1, CAP, 2))(marker_tile_keys, marker_tile_turns).reshape((STEPS, MARKERS, 1))
    return {"populations_in": populations_in, "marker_force": marker_force, "marker_frac": marker_frac, "marker_cell": marker_cell, "marker_tile": marker_tile}


LATTICE = [(0, 0, 0), (1, 0, 0), (-1, 0, 0), (0, 1, 0), (0, -1, 0), (0, 0, 1), (0, 0, -1),
           (1, 1, 0), (-1, -1, 0), (1, -1, 0), (-1, 1, 0), (1, 0, 1), (-1, 0, -1),
           (1, 0, -1), (-1, 0, 1), (0, 1, 1), (0, -1, -1), (0, 1, -1), (0, -1, 1)]
WEIGHTS = [1.0 / 3.0] + [1.0 / 18.0] * 6 + [1.0 / 36.0] * 12
relax_time = 0.8


def lattice_dot(vector, comps, like):
    total = jnp.zeros_like(like)
    for number in range(3):
        if vector[number] == 1:
            total = total + comps[number]
        elif vector[number] == -1:
            total = total - comps[number]
    return total


def moments(fields):
    density = fields[0]
    for member in range(1, 19):
        density = density + fields[member]
    momenta = []
    for number in range(3):
        total = jnp.zeros_like(density)
        for member in range(19):
            if LATTICE[member][number] == 1:
                total = total + fields[member]
            elif LATTICE[member][number] == -1:
                total = total - fields[member]
        momenta.append(total)
    return density, momenta


def velocity_of(fields, force):
    density, momenta = moments(fields)
    return [(momenta[number] + 0.5 * force[number]) / density for number in range(3)]


def collide(fields, force):
    density, momenta = moments(fields)
    speed = [(momenta[number] + 0.5 * force[number]) / density for number in range(3)]
    speed_sq = speed[0] * speed[0] + speed[1] * speed[1] + speed[2] * speed[2]
    along_force = speed[0] * force[0] + speed[1] * force[1] + speed[2] * force[2]
    posts = []
    for member in range(19):
        vector = LATTICE[member]
        project = lattice_dot(vector, speed, density)
        cforce = lattice_dot(vector, force, density)
        equilib = WEIGHTS[member] * density * (1.0 + 3.0 * project + 4.5 * project * project - 1.5 * speed_sq)
        source = (1.0 - 0.5 / relax_time) * WEIGHTS[member] * (3.0 * (cforce - along_force) + 9.0 * project * cforce)
        posts.append(fields[member] - (fields[member] - equilib) / relax_time + source)
    return posts


def reference(populations_in, marker_force, marker_frac, marker_cell, marker_tile):
    fields = [populations_in[member] for member in range(19)]
    outputs = []
    for step in range(STEPS):
        tiles = marker_tile[step, :, 0]
        base_x = (tiles // N_GY) * CX + marker_cell[step, 0]
        base_y = (tiles % N_GY) * CY + marker_cell[step, 1]
        base_z = marker_cell[step, 2]
        frac = marker_frac[step]
        force = marker_force[step]
        corners = []
        for shift_z in range(2):
            weight_z = frac[2] if shift_z else 1.0 - frac[2]
            for shift_x in range(2):
                weight_x = frac[0] if shift_x else 1.0 - frac[0]
                for shift_y in range(2):
                    weight_y = frac[1] if shift_y else 1.0 - frac[1]
                    flat = ((base_z + shift_z) * NX + base_x + shift_x) * NY + base_y + shift_y
                    corners.append((flat.astype(jnp.int32), weight_z * weight_x * weight_y))
        field = jnp.zeros((3, PLANES * NX * NY), jnp.float32)
        for flat, weight in corners:
            field = field.at[:, flat].add(weight[None, :] * force)
        force_field = field.reshape(3, PLANES, NX, NY)
        posts = collide(fields, force_field)
        fields = [jnp.roll(posts[member], (LATTICE[member][2], LATTICE[member][0], LATTICE[member][1]), axis=(0, 1, 2))
                  for member in range(19)]
        probe = jnp.stack(velocity_of(fields, force_field)).reshape(3, -1)
        sampled = jnp.zeros((3, MARKERS), jnp.float32)
        for flat, weight in corners:
            sampled = sampled + weight[None, :] * probe[:, flat]
        outputs.append(sampled)
    return jnp.stack(fields), jnp.stack(outputs)
```

```python
import functools

import jax
import jax.numpy as jnp
from jax import lax
from jax.experimental import pallas as pl
from jax.experimental.pallas import tpu as pltpu
from jax.sharding import PartitionSpec as P

LATTICE = [
    (0, 0, 0),
    (1, 0, 0),
    (-1, 0, 0),
    (0, 1, 0),
    (0, -1, 0),
    (0, 0, 1),
    (0, 0, -1),
    (1, 1, 0),
    (-1, -1, 0),
    (1, -1, 0),
    (-1, 1, 0),
    (1, 0, 1),
    (-1, 0, -1),
    (1, 0, -1),
    (-1, 0, 1),
    (0, 1, 1),
    (0, -1, -1),
    (0, 1, -1),
    (0, -1, 1),
]
WEIGHTS = [1.0 / 3.0] + [1.0 / 18.0] * 6 + [1.0 / 36.0] * 12
TAU = 0.8
CAP = 8
MESH = pl.DeviceIdType.MESH
F32, BF16 = jnp.float32, jnp.bfloat16

XP = [i for i in range(19) if LATTICE[i][0] == 1]
XM = [i for i in range(19) if LATTICE[i][0] == -1]
YP = [i for i in range(19) if LATTICE[i][1] == 1]
YM = [i for i in range(19) if LATTICE[i][1] == -1]


def iota(shape, axis):
    return lax.broadcasted_iota(jnp.int32, shape, axis)


def split2(x):
    hi = x.astype(BF16)
    return hi, (x - hi.astype(F32)).astype(BF16)


def split3(x):
    hi = x.astype(BF16)
    rest = x - hi.astype(F32)
    mid = rest.astype(BF16)
    return hi, mid, (rest - mid.astype(F32)).astype(BF16)


def dot_nt(a, b):
    return lax.dot_general(a, b, (((1,), (1,)), ((), ())), preferred_element_type=F32)


def dot_nn(a, b):
    return jnp.dot(a, b, preferred_element_type=F32)


def moments(f):
    s = {i: f[i] + f[i + 1] for i in range(1, 19, 2)}
    d = {i: f[i] - f[i + 1] for i in range(1, 19, 2)}
    rho = f[0] + (((s[1] + s[3]) + (s[5] + s[7])) + ((s[9] + s[11]) + (s[13] + (s[15] + s[17]))))
    mx = (d[1] + d[7]) + (d[9] + d[11]) + d[13]
    my = (d[3] + d[7]) + (d[15] - d[9]) + d[17]
    mz = (d[5] + d[11]) + (d[15] - d[13]) - d[17]
    return rho, (mx, my, mz)


def along(vector, comps):
    total = None
    for number in range(3):
        if vector[number] == 1:
            total = comps[number] if total is None else total + comps[number]
        elif vector[number] == -1:
            total = -comps[number] if total is None else total - comps[number]
    return total


def collide(f, rho, half, u, force):
    a = rho * (1.0 / TAU)
    big = 1.0 - 0.5 / TAU
    h = [half[n] * (4.5 / TAU) + force[n] * (9.0 * big) for n in range(3)]
    g = [half[n] * (3.0 / TAU) + force[n] * (3.0 * big) for n in range(3)]
    base = a - (u[0] * h[0] + u[1] * h[1] + u[2] * h[2]) * (1.0 / 3.0)
    keep = 1.0 - 1.0 / TAU
    posts = [None] * 19
    posts[0] = f[0] * keep + base * WEIGHTS[0]
    for lead, weight in ((1, WEIGHTS[1]), (7, WEIGHTS[7])):
        wb = base * weight
        wg = [x * weight for x in g]
        wh = [x * weight for x in h]
        for i in range(lead, 7 if lead == 1 else 19, 2):
            even = wb + along(LATTICE[i], u) * along(LATTICE[i], wh)
            odd = along(LATTICE[i], wg)
            posts[i] = f[i] * keep + (even + odd)
            posts[i + 1] = f[i + 1] * keep + (even - odd)
    return posts


def kernel(
    ngx, ngy, pop_hbm, force_hbm, frac_hbm, cell_hbm, tile_hbm, out_hbm, vel_hbm,
    fbuf, pa, pb, mforce, mfrac, mcell, mtile, vout, member, posrow,
    snd0, snd1, sndv, rcv0, rcv1, rcvv, rt, pt, ahi, alo, khi, klo, f0, f1, pr0, pr1, vbuf,
    sx, sy, rx, ry, in_sems, xs_sems, xr_sems, hs_sems, hr_sems, out_sems,
):
    nd = ngx * ngy
    gx, gy = lax.axis_index("gx"), lax.axis_index("gy")
    me = gx * ngy + gy

    mcopies = [
        pltpu.make_async_copy(src, dst, in_sems.at[k])
        for k, (src, dst) in enumerate(
            ((tile_hbm, mtile), (cell_hbm, mcell), (frac_hbm, mfrac), (force_hbm, mforce))
        )
    ]
    for copy in mcopies:
        copy.start()
    popcopy = pltpu.make_async_copy(pop_hbm, fbuf, in_sems.at[4])
    popcopy.start()

    barrier = pltpu.get_barrier_semaphore()

    def greet(k, carry):
        to = lax.rem(me + k, nd)
        pl.semaphore_signal(
            barrier, inc=1, device_id=(to // ngy, lax.rem(to, ngy)), device_id_type=MESH
        )
        return carry

    lax.fori_loop(1, nd, greet, 0)
    if nd < 128:
        for ref in (rcv0, rcv1, rcvv):
            ref[...] = jnp.zeros_like(ref)
    vbuf[...] = jnp.zeros_like(vbuf)

    for copy in mcopies:
        copy.wait()

    owned = mtile.shape[2]
    before = jnp.where(iota((owned, owned), 0) < iota((owned, owned), 1), 1.0, 0.0).astype(BF16)

    def pack(step, snd):
        ids = iota((128, owned), 0).astype(F32)
        tiles = mtile[step].astype(F32)
        hit = jnp.where(ids == tiles, 1.0, 0.0)
        hit16 = hit.astype(BF16)
        member[step] = hit16
        position = jnp.sum(dot_nn(hit16, before) * hit, axis=0, keepdims=True)
        posrow[step] = position
        mine = iota((CAP, owned), 0).astype(F32) == position
        rows = []
        for ref in (mcell, mfrac, mforce):
            for n in range(3):
                value = ref[n, pl.ds(step, 1), :].astype(F32)
                rows.append(jnp.where(mine, value, 0.0))
        rows.append(jnp.zeros((128 - 9 * CAP, owned), F32))
        x = jnp.concatenate(rows, axis=0)
        hi, mid, lo = split3(x)
        y = dot_nt(hit16, hi) + (dot_nt(hit16, mid) + dot_nt(hit16, lo))
        snd[...] = y.reshape(128, 1, 128)

    def exchange(snd, rcv, which):
        own = pltpu.make_async_copy(snd.at[me], rcv.at[me], xr_sems.at[which])
        own.start()

        def send(k, carry):
            to = lax.rem(me + k, nd)
            pltpu.make_async_remote_copy(
                src_ref=snd.at[to],
                dst_ref=rcv.at[me],
                send_sem=xs_sems.at[which],
                recv_sem=xr_sems.at[which],
                device_id=(to // ngy, lax.rem(to, ngy)),
                device_id_type=MESH,
            ).start()
            return carry

        lax.fori_loop(1, nd, send, 0)

    def arrived(rcv, which):
        pltpu.make_async_copy(
            rcv.at[pl.ds(0, nd)], rcv.at[pl.ds(0, nd)], xr_sems.at[which]
        ).wait()

    def departed(snd, which):
        pltpu.make_async_copy(
            snd.at[pl.ds(0, nd - 1)], snd.at[pl.ds(0, nd - 1)], xs_sems.at[which]
        ).wait()

    pack(0, snd0)
    pl.semaphore_wait(barrier, nd - 1)
    exchange(snd0, rcv0, 0)
    pack(1, snd1)
    exchange(snd1, rcv1, 1)

    def spread(step, rcv, fout):
        rt[...] = rcv[...].reshape(128, 128).T
        zx = iota((128, 128), 0)
        xs = (zx & 31).astype(F32)
        zs = (zx >> 5).astype(F32)
        ys = iota((384, 128), 0).astype(F32)

        def table(j, carry):
            def row(v):
                return rt[pl.ds(v * CAP + j, 1), :]

            cx, cy, cz, fx, fy, fz = [row(v) for v in range(6)]
            dx, dy, dz = xs - cx, ys - cy, zs - cz
            wx = jnp.where(dx == 0.0, 1.0 - fx, jnp.where(dx == 1.0, fx, 0.0))
            wz = jnp.where(dz == 0.0, 1.0 - fz, jnp.where(dz == 1.0, fz, 0.0))
            w = wz * wx
            lanes = pl.ds(pl.multiple_of(j * 128, 128), 128)
            pt[step, :, lanes] = w
            for n in range(3):
                hi, lo = split2(w * row(6 + n))
                ahi[pl.ds(n * 128, 128), lanes] = hi
                alo[pl.ds(n * 128, 128), lanes] = lo
            wy = jnp.where(dy == 0.0, 1.0 - fy, jnp.where(dy == 1.0, fy, 0.0))
            hi, lo = split2(wy)
            khi[step, :, lanes] = hi
            klo[step, :, lanes] = lo
            return carry

        lax.fori_loop(0, CAP, table, 0)
        for n in range(3):
            rows = pl.ds(n * 128, 128)
            a, b = ahi[rows, :], alo[rows, :]
            fout[rows, :] = dot_nt(a, khi[step]) + (dot_nt(a, klo[step]) + dot_nt(b, khi[step]))

    def sample(step, probe):
        def body(j, carry):
            lanes = pl.ds(pl.multiple_of(j * 256, 256), 256)
            kh, kl = khi[step, :, lanes], klo[step, :, lanes]
            w = pt[step, :, lanes]
            for n in range(3):
                hi, lo = split2(probe[pl.ds(n * 128, 128), :])
                s = dot_nn(hi, kh) + (dot_nn(hi, kl) + dot_nn(lo, kh))
                r = jnp.sum(s * w, axis=0, keepdims=True)
                base = step * 3 * CAP + n * CAP
                vbuf[pl.ds(base + 2 * j, 1), :] = r[:, 0:128]
                vbuf[pl.ds(base + 2 * j + 1, 1), :] = r[:, 128:256]
            return carry

        lax.fori_loop(0, CAP // 2, body, 0)

    def place(dx, dy):
        return lax.rem(gx + dx + ngx, ngx), lax.rem(gy + dy + ngy, ngy)

    def halo_copies(phase):
        plan = [
            (sx.at[phase, 0], rx.at[phase, 0], (1, 0)),
            (sx.at[phase, 1], rx.at[phase, 1], (-1, 0)),
            (sy.at[phase, 0], ry.at[phase, 2], (1, 1)),
            (sy.at[phase, 0], ry.at[phase, 3], (-1, 1)),
            (sy.at[phase, 1], ry.at[phase, 4], (-1, -1)),
            (sy.at[phase, 1], ry.at[phase, 5], (1, -1)),
            (sy.at[phase, 0], ry.at[phase, 0], (0, 1)),
            (sy.at[phase, 1], ry.at[phase, 1], (0, -1)),
        ]
        return [
            pltpu.make_async_remote_copy(
                src_ref=src,
                dst_ref=dst,
                send_sem=hs_sems.at[phase, k],
                recv_sem=hr_sems.at[phase, k],
                device_id=place(*to),
                device_id_type=MESH,
            )
            for k, (src, dst, to) in enumerate(plan)
        ]

    def halo_send(phase, post):
        copies = halo_copies(phase)
        for k in range(5):
            for z in range(4):
                sx[phase, 0, k, z] = post[XP[k], z, 39:40, 128:512]
                sx[phase, 1, k, z] = post[XM[k], z, 8:9, 128:512]
        copies[0].start()
        copies[1].start()
        lane = iota((128, 128), 1)
        packed = jnp.zeros((128, 128), F32)
        for k in range(5):
            high = post[YP[k], :, 8:40, 384:512].reshape(128, 128)
            low = post[YM[k], :, 8:40, 128:256].reshape(128, 128)
            packed = jnp.where(lane == k, pltpu.roll(high, k + 1, 1), packed)
            packed = jnp.where(lane == 8 + k, pltpu.roll(low, 8 + k, 1), packed)
        rows = packed.T
        sy[phase, 0] = rows[0:8, :]
        sy[phase, 1] = rows[8:16, :]
        for copy in copies[2:]:
            copy.start()
        return copies

    def halo_take(phase, post, copies):
        for copy in copies:
            copy.wait_recv()
        for k in range(5):
            for z in range(4):
                post[XP[k], z, 7:8, 128:512] = rx[phase, 0, k, z]
                post[XM[k], z, 40:41, 128:512] = rx[phase, 1, k, z]
        w = jnp.concatenate(
            [ry[phase].reshape(48, 128), jnp.zeros((80, 128), F32)], axis=0
        ).T
        for k in range(5):
            post[YP[k], :, 8:40, 0:128] = pltpu.roll(w, 127 - k, 1).reshape(4, 32, 128)
            post[YM[k], :, 8:40, 512:640] = pltpu.roll(w, 120 - k, 1).reshape(4, 32, 128)
        for i, slot, row, src, dst, side in (
            (7, 2, 1, 24, 0, 0),
            (10, 3, 2, 0, 40, 0),
            (8, 4, 1, 0, 40, 1),
            (9, 5, 2, 24, 0, 1),
        ):
            shift = ((0 if side else 127) - (8 * slot + row)) % 128
            for z in range(4):
                part = w[z * 32 + src : z * 32 + src + 8, :]
                post[i, z, dst : dst + 8, side * 512 : side * 512 + 128] = pltpu.roll(part, shift, 1)

    def chunk_of(c):
        z, rest = c // 12, lax.rem(c, 12)
        return z, rest // 3, lax.rem(rest, 3)

    def forces(ref, z, xt, l):
        lanes = pl.ds(pl.multiple_of(l * 128, 128), 128)
        return [
            ref[pl.ds(pl.multiple_of(n * 128 + z * 32 + xt * 8, 8), 8), lanes] for n in range(3)
        ]

    def put3(ref, z, xt, l, values):
        lanes = pl.ds(pl.multiple_of(l * 128, 128), 128)
        for n in range(3):
            ref[pl.ds(pl.multiple_of(n * 128 + z * 32 + xt * 8, 8), 8), lanes] = values[n]

    def streamed(post, z, xt, l):
        sub, lane = iota((8, 128), 0), iota((8, 128), 1)

        def load(i, zz, rows, cols):
            return post[
                i,
                zz,
                pl.ds(pl.multiple_of(8 + xt * 8 + 8 * rows, 8), 8),
                pl.ds(pl.multiple_of(128 + l * 128 + 128 * cols, 128), 128),
            ]

        fields = []
        for i in range(19):
            vx, vy, vz = LATTICE[i]
            zz = z if vz == 0 else lax.rem(z + (3 if vz == 1 else 1), 4)

            def across(rows):
                value = load(i, zz, rows, 0)
                if vy == 1:
                    value = jnp.where(lane == 127, load(i, zz, rows, -1), value)
                elif vy == -1:
                    value = jnp.where(lane == 0, load(i, zz, rows, 1), value)
                return value

            value = across(0)
            if vx == 1:
                value = jnp.where(sub == 7, across(-1), value)
            elif vx == -1:
                value = jnp.where(sub == 0, across(1), value)
            if vx != 0:
                value = pltpu.roll(value, 1 if vx == 1 else 7, 0)
            if vy != 0:
                value = pltpu.roll(value, 1 if vy == 1 else 127, 1)
            fields.append(value)
        return fields

    def store_posts(post, z, xt, l, values):
        rows = pl.ds(pl.multiple_of(8 + xt * 8, 8), 8)
        lanes = pl.ds(pl.multiple_of(128 + l * 128, 128), 128)
        for i in range(19):
            post[i, z, rows, lanes] = values[i]

    def first(c, carry):
        z, xt, l = chunk_of(c)
        rows = pl.ds(pl.multiple_of(xt * 8, 8), 8)
        lanes = pl.ds(pl.multiple_of(l * 128, 128), 128)
        f = [fbuf[i, z, rows, lanes] for i in range(19)]
        force = forces(f0, z, xt, l)
        rho, m = moments(f)
        inv = 1.0 / rho
        half = [m[n] + 0.5 * force[n] for n in range(3)]
        u = [half[n] * inv for n in range(3)]
        store_posts(pa, z, xt, l, collide(f, rho, half, u, force))
        return carry

    def second(c, carry):
        z, xt, l = chunk_of(c)
        f = streamed(pa, z, xt, l)
        old, force = forces(f0, z, xt, l), forces(f1, z, xt, l)
        rho, m = moments(f)
        inv = 1.0 / rho
        put3(pr0, z, xt, l, [(m[n] + 0.5 * old[n]) * inv for n in range(3)])
        half = [m[n] + 0.5 * force[n] for n in range(3)]
        u = [half[n] * inv for n in range(3)]
        store_posts(pb, z, xt, l, collide(f, rho, half, u, force))
        return carry

    def third(c, carry):
        z, xt, l = chunk_of(c)
        f = streamed(pb, z, xt, l)
        rows = pl.ds(pl.multiple_of(xt * 8, 8), 8)
        lanes = pl.ds(pl.multiple_of(l * 128, 128), 128)
        for i in range(19):
            fbuf[i, z, rows, lanes] = f[i]
        force = forces(f1, z, xt, l)
        rho, m = moments(f)
        inv = 1.0 / rho
        put3(pr1, z, xt, l, [(m[n] + 0.5 * force[n]) * inv for n in range(3)])
        return carry

    arrived(rcv0, 0)
    spread(0, rcv0, f0)
    popcopy.wait()
    lax.fori_loop(0, 48, first, 0)
    halo0 = halo_send(0, pa)
    arrived(rcv1, 1)
    spread(1, rcv1, f1)
    halo_take(0, pa, halo0)
    lax.fori_loop(0, 48, second, 0)
    halo1 = halo_send(1, pb)
    sample(0, pr0)
    halo_take(1, pb, halo1)
    lax.fori_loop(0, 48, third, 0)
    outcopy = pltpu.make_async_copy(fbuf, out_hbm, out_sems.at[0])
    outcopy.start()
    sample(1, pr1)
    sndv[...] = vbuf[...].T.reshape(128, 1, 128)
    exchange(sndv, rcvv, 2)
    arrived(rcvv, 2)

    back = rcvv[...].reshape(128, 128).T
    for step in range(2):
        rows = back[step * 3 * CAP : (step + 1) * 3 * CAP, :]
        hit = member[step]
        hi, mid, lo = split3(rows)
        g = dot_nn(hi, hit) + (dot_nn(mid, hit) + dot_nn(lo, hit))
        mine = iota((CAP, owned), 0).astype(F32) == posrow[step]
        for n in range(3):
            own = jnp.where(mine, g[n * CAP : (n + 1) * CAP, :], 0.0)
            vout[n, pl.ds(step, 1), :] = jnp.sum(own, axis=0, keepdims=True)
    velcopy = pltpu.make_async_copy(vout, vel_hbm, out_sems.at[1])
    velcopy.start()

    departed(snd0, 0)
    departed(snd1, 1)
    departed(sndv, 2)
    for copy in halo0 + halo1:
        copy.wait_send()
    outcopy.wait()
    velcopy.wait()


def local(populations_in, marker_force, marker_frac, marker_cell, marker_tile):
    ngx, ngy = lax.axis_size("gx"), lax.axis_size("gy")
    owned = marker_force.shape[2]
    steps = marker_force.shape[0]
    slots = 128 * CAP
    vm = pltpu.VMEM
    row3 = vm((128, 1, 128), F32)
    anywhere = pl.BlockSpec(memory_space=pl.ANY)
    fields, velocity = pl.pallas_call(
        functools.partial(kernel, ngx, ngy),
        out_shape=(
            jax.ShapeDtypeStruct(populations_in.shape, F32),
            jax.ShapeDtypeStruct((3, steps, owned), F32),
        ),
        in_specs=[anywhere] * 5,
        out_specs=(anywhere, anywhere),
        scratch_shapes=[
            vm((19, 4, 32, 384), F32),
            vm((19, 4, 48, 640), F32),
            vm((19, 4, 48, 640), F32),
            vm((3, steps, owned), F32),
            vm((3, steps, owned), F32),
            vm((3, steps, owned), jnp.int32),
            vm((steps, 1, owned), jnp.int32),
            vm((3, steps, owned), F32),
            vm((steps, 128, owned), BF16),
            vm((steps, 1, owned), F32),
            row3, row3, row3, row3, row3, row3,
            vm((128, 128), F32),
            vm((2, 128, slots), F32),
            vm((384, slots), BF16),
            vm((384, slots), BF16),
            vm((2, 384, slots), BF16),
            vm((2, 384, slots), BF16),
            vm((384, 384), F32),
            vm((384, 384), F32),
            vm((384, 384), F32),
            vm((384, 384), F32),
            vm((128, 128), F32),
            vm((2, 2, 5, 4, 1, 384), F32),
            vm((2, 2, 8, 128), F32),
            vm((2, 2, 5, 4, 1, 384), F32),
            vm((2, 6, 8, 128), F32),
            pltpu.SemaphoreType.DMA((5,)),
            pltpu.SemaphoreType.DMA((3,)),
            pltpu.SemaphoreType.DMA((3,)),
            pltpu.SemaphoreType.DMA((2, 8)),
            pltpu.SemaphoreType.DMA((2, 8)),
            pltpu.SemaphoreType.DMA((2,)),
        ],
        compiler_params=pltpu.CompilerParams(
            collective_id=0, has_side_effects=True, vmem_limit_bytes=60 * 1024 * 1024
        ),
    )(
        populations_in,
        jnp.transpose(marker_force, (1, 0, 2)),
        jnp.transpose(marker_frac, (1, 0, 2)),
        jnp.transpose(marker_cell, (1, 0, 2)),
        jnp.transpose(marker_tile, (0, 2, 1)),
    )
    return fields, jnp.transpose(velocity, (1, 0, 2))


def solution(mesh):
    return jax.shard_map(
        local,
        mesh=mesh,
        in_specs=(
            P(None, None, "gx", "gy"),
            P(None, None, ("gx", "gy")),
            P(None, None, ("gx", "gy")),
            P(None, None, ("gx", "gy")),
            P(None, ("gx", "gy"), None),
        ),
        out_specs=(P(None, None, "gx", "gy"), P(None, None, ("gx", "gy"))),
        check_vma=False,
    )
```
